32 devices in a mesh: dp: 8 (over z, core), chan: 4 (over y, x).
Axes of the slice: x: 2, y: 2, z: 4, core: 2. Of those that a mesh axis runs over, the one named last changes fastest.
Arguments:
- images: bfloat16 [16, 16, 16, 2816], P('dp', None, None, 'chan'), may hold values from -6 to 6
- kernel: float32 [7, 7, 2816], P(None, None, 'chan'), may hold values from -0.875 to 0.875
- layernorm_gain: float32 [2816], P('chan'), may hold values from 0.25 to 1.75
- layernorm_bias: float32 [2816], P('chan'), may hold values from -3 to 3
- w_expand: bfloat16 [2816, 11264], P('dp', 'chan'), may hold values from -0.109375 to 0.109375
- w_reduce: bfloat16 [11264, 2816], P('chan', 'dp'), may hold values from -0.0546875 to 0.0546875
- layer_scale: float32 [2816], P('chan'), may hold values from 0.25 to 1
- cotangent: bfloat16 [16, 16, 16, 2816], P('dp', None, None, 'chan'), may hold values from -6 to 6
Outputs:
- output: bfloat16 [16, 16, 16, 2816], P('dp', None, None, 'chan')
- grad_images: bfloat16 [16, 16, 16, 2816], P('dp', None, None, 'chan')
- grad_kernel: float32 [7, 7, 2816], P(None, None, 'chan')
- gain_gradient: float32 [2816], P('chan')
- grad_bias: float32 [2816], P('chan')
- grad_expand: float32 [2816, 11264], P('dp', 'chan')
- grad_reduce: float32 [11264, 2816], P('chan', 'dp')
- grad_scale: float32 [2816], P('chan')
The draws below stay inside these ranges and needn't reach their ends.
All inputs are finite; a program needn't handle non-finite values.
Results may differ from the reference program's by a relative error of at most 0.025.
Values may be sent and summed in bfloat16 or wider, within the bound.
A program may use at most 128 MiB of HBM per device.

```python
import math
import jax
import jax.numpy as jnp
from jax import lax

C = 2816
FF = 11264
KS = 7
IMG_DEV = 2
HH = 16
WW = 16
IMAGES = 16
N_DP = 8
N_CHAN = 4


def with_spikes(entries, stream_key, source, target, parts, factor):
    owner, partner = [(jnp.arange(entries.shape[axis_at]) // (entries.shape[axis_at] // parts)).reshape([-1 if axis == axis_at else 1 for axis in range(entries.ndim)]) for axis_at in (source, target)]
    chosen = jax.random.permutation(stream_key, parts)[partner]
    strong = (owner == chosen) | (owner == (partner + parts // 2) % parts)
    return jnp.where(strong, factor * entries, entries)


def levels(own_key, shape, cuts, low, high):
    def one(dim, shards_of):
        draws = jax.random.uniform(jax.random.fold_in(jax.random.fold_in(own_key, 6), dim), (shards_of,), jnp.float32, low / len(cuts), high / len(cuts))
        return jnp.repeat(jnp.exp(draws), shape[dim] // shards_of).reshape((-1,) + (1,) * (len(shape) - dim - 1))

    gain = one(*cuts[0])
    for cut in cuts[1:]:
        gain = gain * one(*cut)
    return gain


def gaussian(stream_key, shape, width, reach, split=(), dtype=jnp.bfloat16):
    values = width * jax.random.normal(stream_key, shape, jnp.float32)
    if split:
        values = values * levels(stream_key, shape, split, -0.22, 0.18)
    return jnp.clip(values, -reach, reach).astype(dtype)


def gaussian_with(rng, dims, deviation, limit, pieces, heavy, kind=jnp.bfloat16):
    values = deviation * jax.random.normal(rng, dims, jnp.float32)
    if pieces:
        values = values * levels(rng, dims, pieces, -0.22, 0.18)
    return jnp.clip(with_spikes(values, jax.random.fold_in(rng, 3), *heavy), -limit, limit).astype(kind)


def setup_inputs(seed: int = 0) -> dict:
    key_of = jax.random.split(jax.random.key(seed), 9)
    images = gaussian(key_of[0], (IMAGES, HH, WW, C), 1.0, 6.0, ((0, 8), (3, 4)))
    kernel = gaussian(key_of[1], (KS, KS, C), (KS * KS) ** -0.5, 0.875, ((2, 4),), jnp.float32)
    layernorm_gain = jnp.clip(1.0 + 0.15 * jax.random.normal(key_of[2], (C,), jnp.float32), 0.25, 1.75)
    layernorm_bias = gaussian(key_of[3], (C,), 0.5, 3.0, ((0, 4),), jnp.float32)
    w_expand = gaussian(key_of[4], (C, FF), C ** -0.5, 0.109375, ((0, 8), (1, 4)))
    w_reduce = gaussian(key_of[5], (FF, C), FF ** -0.5, 0.0546875, ((0, 4), (1, 8)))
    layer_scale = jnp.clip(jnp.exp(math.log(1.0) - 1.3862944 * jax.random.uniform(key_of[6], (C,), jnp.float32) ** levels(key_of[6], (C,), ((0, 4),), -0.2, 0.2)), 0.25, 1.0)
    cotangent = gaussian_with(key_of[7], (IMAGES, HH, WW, C), 1.0, 6.0, ((0, 8), (3, 4)), (0, 3, 8, 2.0))
    return dict(images=images, kernel=kernel, layernorm_gain=layernorm_gain, layernorm_bias=layernorm_bias, w_expand=w_expand, w_reduce=w_reduce, layer_scale=layer_scale, cotangent=cotangent)


eps = 1e-06

def depthwise(field, kern):
    padded = jnp.pad(field, ((0, 0), (3, 3), (3, 3), (0, 0)))
    total = jnp.zeros(field.shape, jnp.float32)
    for i in range(KS):
        for j in range(KS):
            total = total + padded[:, i:i + HH, j:j + WW, :] * kern[i, j]
    return total

def normal_cdf(value):
    return 0.5 * (1.0 + jax.scipy.special.erf(value / math.sqrt(2.0)))

def rounded(value):
    return lax.optimization_barrier(value.astype(jnp.bfloat16)).astype(jnp.float32)

def reference(images, kernel, layernorm_gain, layernorm_bias, w_expand, w_reduce, layer_scale, cotangent):
    xf = images.astype(jnp.float32)
    conv = depthwise(xf, kernel).reshape(-1, C)
    mean_val = lax.optimization_barrier(jnp.mean(conv, axis=1, keepdims=True))
    centred_rows = conv - mean_val
    var = lax.optimization_barrier(jnp.mean(centred_rows * centred_rows, axis=1, keepdims=True))
    inverse_deviation = lax.rsqrt(var + eps)
    standardized_input = centred_rows * inverse_deviation
    normed_output = (standardized_input * layernorm_gain + layernorm_bias).astype(jnp.bfloat16)
    pre = jnp.dot(normed_output, w_expand, preferred_element_type=jnp.float32)
    hidden = (pre * normal_cdf(pre)).astype(jnp.bfloat16)
    group = FF // N_CHAN
    branch = jnp.zeros(conv.shape, jnp.float32)
    for g in range(N_CHAN):
        branch = branch + rounded(jnp.dot(hidden[:, g * group:(g + 1) * group], w_reduce[g * group:(g + 1) * group], preferred_element_type=jnp.float32))
    xr = xf.reshape(-1, C)
    output = (xr + layer_scale * branch).astype(jnp.bfloat16).reshape(images.shape)
    dyf = cotangent.astype(jnp.float32).reshape(-1, C)
    grad_scale = lax.optimization_barrier(jnp.sum(dyf * branch, axis=0))
    dbranch = (dyf * layer_scale).astype(jnp.bfloat16)
    rows = IMG_DEV * HH * WW
    grad_reduce = jnp.zeros((FF, C), jnp.float32)
    for p in range(N_DP):
        grad_reduce = grad_reduce + rounded(jnp.dot(hidden[p * rows:(p + 1) * rows].T, dbranch[p * rows:(p + 1) * rows], preferred_element_type=jnp.float32))
    dhidden = jnp.dot(dbranch, w_reduce.T, preferred_element_type=jnp.float32)
    slope = normal_cdf(pre) + pre * jnp.exp(-0.5 * pre * pre) / math.sqrt(2.0 * math.pi)
    dpre = (dhidden * slope).astype(jnp.bfloat16)
    grad_expand = jnp.zeros((C, FF), jnp.float32)
    for p in range(N_DP):
        grad_expand = grad_expand + rounded(jnp.dot(normed_output[p * rows:(p + 1) * rows].T, dpre[p * rows:(p + 1) * rows], preferred_element_type=jnp.float32))
    normed_grad = jnp.zeros(conv.shape, jnp.float32)
    for g in range(N_CHAN):
        normed_grad = normed_grad + rounded(jnp.dot(dpre[:, g * group:(g + 1) * group], w_expand[:, g * group:(g + 1) * group].T, preferred_element_type=jnp.float32))
    gain_gradient = lax.optimization_barrier(jnp.sum(normed_grad * standardized_input, axis=0))
    grad_bias = lax.optimization_barrier(jnp.sum(normed_grad, axis=0))
    standardized_grad = normed_grad * layernorm_gain
    first_half = lax.optimization_barrier(jnp.mean(standardized_grad, axis=1, keepdims=True))
    second_half = lax.optimization_barrier(jnp.mean(standardized_grad * standardized_input, axis=1, keepdims=True))
    conv_output_grad = (inverse_deviation * (standardized_grad - first_half - standardized_input * second_half)).reshape(images.shape)
    padded = jnp.pad(xf, ((0, 0), (3, 3), (3, 3), (0, 0)))
    dpad = jnp.pad(conv_output_grad, ((0, 0), (3, 3), (3, 3), (0, 0)))
    kern_rows = []
    back = cotangent.astype(jnp.float32)
    for i in range(KS):
        tap_row = []
        for j in range(KS):
            tap_row.append(lax.optimization_barrier(jnp.sum(padded[:, i:i + HH, j:j + WW, :] * conv_output_grad, axis=(0, 1, 2))))
            back = back + dpad[:, 6 - i:6 - i + HH, 6 - j:6 - j + WW, :] * kernel[i, j]
        kern_rows.append(jnp.stack(tap_row))
    grad_kernel = jnp.stack(kern_rows)
    grad_images = back.astype(jnp.bfloat16)
    return (output, grad_images, grad_kernel, gain_gradient, grad_bias, grad_expand, grad_reduce, grad_scale)
```

```python
import math

import jax
import jax.numpy as jnp
from jax import lax
from jax.sharding import PartitionSpec as P

eps = 1e-06


def depthwise(field, kern):
    height = field.shape[1]
    breadth = field.shape[2]
    padded = jnp.pad(field, ((0, 0), (3, 3), (3, 3), (0, 0)))
    total = jnp.zeros(field.shape, jnp.float32)
    for i in range(7):
        for j in range(7):
            total = total + padded[:, i : i + height, j : j + breadth, :] * kern[i, j]
    return total


def normal_cdf(value):
    return 0.5 * (1.0 + jax.scipy.special.erf(value / math.sqrt(2.0)))


def swap_pairs(shift, n):
    return [(i, i ^ shift) for i in range(n)]


def chan_gather(block):
    n = lax.axis_size("chan")
    me = lax.axis_index("chan")
    width = block.shape[1]
    whole = jnp.zeros((block.shape[0], n * width), block.dtype)
    parts = [block] + [lax.ppermute(block, "chan", swap_pairs(k, n)) for k in range(1, n)]
    for k in range(n):
        whole = lax.dynamic_update_slice(whole, parts[k], (0, (me ^ k) * width))
    return whole


def chan_scatter(partial):
    n = lax.axis_size("chan")
    me = lax.axis_index("chan")
    width = partial.shape[1] // n
    total = lax.dynamic_slice_in_dim(partial, me * width, width, 1).astype(jnp.float32)
    for k in range(1, n):
        mine = lax.dynamic_slice_in_dim(partial, (me ^ k) * width, width, 1)
        total = total + lax.ppermute(mine, "chan", swap_pairs(k, n)).astype(jnp.float32)
    return total


def dp_scatter(partial):
    return lax.psum_scatter(partial, "dp", scatter_dimension=0, tiled=True)


def dp_total(value):
    n = lax.axis_size("dp")
    shift = 1
    while shift < n:
        value = value + lax.ppermute(value, "dp", swap_pairs(shift, n))
        shift *= 2
    return value


def body(
    images, kernel, layernorm_gain, layernorm_bias, w_expand, w_reduce, layer_scale, cotangent
):
    shape_in = images.shape
    height = shape_in[1]
    breadth = shape_in[2]
    positions = shape_in[0] * height * breadth
    local_chan = shape_in[3]
    image_width = local_chan * lax.axis_size("chan")
    xf = images.astype(jnp.float32)
    conv = depthwise(xf, kernel).reshape(positions, local_chan)
    mean_val = lax.psum(jnp.sum(conv, axis=1), "chan")[:, None] / image_width
    centred_rows = conv - mean_val
    var = lax.psum(jnp.sum(centred_rows * centred_rows, axis=1), "chan")[:, None] / image_width
    inverse_deviation = lax.rsqrt(var + eps)
    standardized_input = centred_rows * inverse_deviation
    normed_output = (standardized_input * layernorm_gain + layernorm_bias).astype(jnp.bfloat16)
    normed_all = chan_gather(normed_output)
    expand_all = lax.all_gather(w_expand, "dp", axis=0, tiled=True)
    pre = jnp.dot(normed_all, expand_all, preferred_element_type=jnp.float32)
    hidden = (pre * normal_cdf(pre)).astype(jnp.bfloat16)
    dyf = cotangent.astype(jnp.float32).reshape(positions, local_chan)
    dbranch = (dyf * layer_scale).astype(jnp.bfloat16)
    dbranch_all = chan_gather(dbranch)
    reduce_part = lax.dot_general(
        dbranch_all, hidden, (((0,), (0,)), ((), ())), preferred_element_type=jnp.float32
    ).astype(jnp.bfloat16)
    reduce_all = lax.all_gather(w_reduce, "dp", axis=1, tiled=True)
    reduce_part, reduce_all = lax.optimization_barrier((reduce_part, reduce_all))
    grad_reduce = dp_scatter(reduce_part).astype(jnp.float32).T
    dhidden = lax.dot_general(
        dbranch_all, reduce_all, (((1,), (1,)), ((), ())), preferred_element_type=jnp.float32
    )
    slope = normal_cdf(pre) + pre * jnp.exp(-0.5 * pre * pre) / math.sqrt(2.0 * math.pi)
    dpre = (dhidden * slope).astype(jnp.bfloat16)
    expand_part = lax.dot_general(
        normed_all, dpre, (((0,), (0,)), ((), ())), preferred_element_type=jnp.float32
    ).astype(jnp.bfloat16)
    expand_part, dpre, hidden, reduce_all = lax.optimization_barrier(
        (expand_part, dpre, hidden, reduce_all)
    )
    grad_expand = dp_scatter(expand_part).astype(jnp.float32)
    partial_normed = lax.dot_general(
        dpre, expand_all, (((1,), (1,)), ((), ())), preferred_element_type=jnp.float32
    )
    normed_grad = chan_scatter(partial_normed.astype(jnp.bfloat16))
    partial_branch = jnp.dot(hidden, reduce_all, preferred_element_type=jnp.float32)
    branch = chan_scatter(partial_branch.astype(jnp.bfloat16))
    xr = xf.reshape(positions, local_chan)
    output = (xr + layer_scale * branch).astype(jnp.bfloat16).reshape(shape_in)
    scale_part = jnp.sum(dyf * branch, axis=0)
    gain_partial = jnp.sum(normed_grad * standardized_input, axis=0)
    bias_part = jnp.sum(normed_grad, axis=0)
    standardized_grad = normed_grad * layernorm_gain
    first_half, second_half = lax.psum(
        (
            jnp.sum(standardized_grad, axis=1),
            jnp.sum(standardized_grad * standardized_input, axis=1),
        ),
        "chan",
    )
    conv_output_grad = inverse_deviation * (
        standardized_grad
        - first_half[:, None] / image_width
        - standardized_input * (second_half[:, None] / image_width)
    )
    conv_output_grad = conv_output_grad.reshape(shape_in)
    padded = jnp.pad(xf, ((0, 0), (3, 3), (3, 3), (0, 0)))
    dpad = jnp.pad(conv_output_grad, ((0, 0), (3, 3), (3, 3), (0, 0)))
    back = cotangent.astype(jnp.float32)
    kern_rows = []
    for i in range(7):
        tap_row = []
        for j in range(7):
            tap_row.append(
                jnp.sum(
                    padded[:, i : i + height, j : j + breadth, :] * conv_output_grad, axis=(0, 1, 2)
                )
            )
            back = back + dpad[:, 6 - i : 6 - i + height, 6 - j : 6 - j + breadth, :] * kernel[i, j]
        kern_rows.append(jnp.stack(tap_row))
    kernel_part = jnp.stack(kern_rows)
    grad_images = back.astype(jnp.bfloat16)
    small = dp_total(
        jnp.concatenate(
            [
                kernel_part.reshape(-1, local_chan),
                gain_partial[None],
                bias_part[None],
                scale_part[None],
            ]
        )
    )
    taps = kernel_part.shape[0] * kernel_part.shape[1]
    grad_kernel = small[:taps].reshape(kernel_part.shape)
    gain_gradient, grad_bias, grad_scale = small[taps], small[taps + 1], small[taps + 2]
    return (
        output,
        grad_images,
        grad_kernel,
        gain_gradient,
        grad_bias,
        grad_expand,
        grad_reduce,
        grad_scale,
    )


def solution(mesh):
    in_specs = (
        P("dp", None, None, "chan"),
        P(None, None, "chan"),
        P("chan"),
        P("chan"),
        P("dp", "chan"),
        P("chan", "dp"),
        P("chan"),
        P("dp", None, None, "chan"),
    )
    out_specs = (
        P("dp", None, None, "chan"),
        P("dp", None, None, "chan"),
        P(None, None, "chan"),
        P("chan"),
        P("chan"),
        P("dp", "chan"),
        P("chan", "dp"),
        P("chan"),
    )
    return jax.shard_map(body, mesh=mesh, in_specs=in_specs, out_specs=out_specs, check_vma=False)
```

```python
import math

import jax
import jax.numpy as jnp
from jax import lax
from jax.sharding import PartitionSpec as P

eps = 1e-06


def depthwise(field, kern):
    height = field.shape[1]
    breadth = field.shape[2]
    padded = jnp.pad(field, ((0, 0), (3, 3), (3, 3), (0, 0)))
    total = jnp.zeros(field.shape, jnp.float32)
    for i in range(7):
        for j in range(7):
            total = total + padded[:, i : i + height, j : j + breadth, :] * kern[i, j]
    return total


def normal_cdf(value):
    return 0.5 * (1.0 + jax.scipy.special.erf(value / math.sqrt(2.0)))


def swap_pairs(shift, n):
    return [(i, i ^ shift) for i in range(n)]


def chan_gather(block):
    n = lax.axis_size("chan")
    me = lax.axis_index("chan")
    width = block.shape[1]
    whole = jnp.zeros((block.shape[0], n * width), block.dtype)
    parts = [block] + [lax.ppermute(block, "chan", swap_pairs(k, n)) for k in range(1, n)]
    for k in range(n):
        whole = lax.dynamic_update_slice(whole, parts[k], (0, (me ^ k) * width))
    return whole


def chan_scatter(partial):
    n = lax.axis_size("chan")
    me = lax.axis_index("chan")
    width = partial.shape[1] // n
    total = lax.dynamic_slice_in_dim(partial, me * width, width, 1).astype(jnp.float32)
    for k in range(1, n):
        mine = lax.dynamic_slice_in_dim(partial, (me ^ k) * width, width, 1)
        total = total + lax.ppermute(mine, "chan", swap_pairs(k, n)).astype(jnp.float32)
    return total


def dp_scatter(partial):
    return lax.psum_scatter(partial, "dp", scatter_dimension=0, tiled=True)


def dp_line_scatter(partial, early):
    n = lax.axis_size("dp")
    m = n // 2
    me = lax.axis_index("dp")
    place, side = me // 2, me % 2
    blocks = partial.reshape(m, 2, partial.shape[0] // n, partial.shape[1])
    own = lax.dynamic_index_in_dim(blocks, side, 1, keepdims=False)
    other = lax.dynamic_index_in_dim(blocks, 1 - side, 1, keepdims=False)
    own = own + lax.ppermute(other, "dp", swap_pairs(1, n))
    up = down = None
    for distance in range(m - 1, 0, -1):
        high = lax.dynamic_index_in_dim(
            own, jnp.minimum(place + distance, m - 1), 0, keepdims=False
        )
        low = lax.dynamic_index_in_dim(own, jnp.maximum(place - distance, 0), 0, keepdims=False)
        if up is not None:
            high, low = high + up, low + down
        senders = range(2 * (m - distance))
        up = lax.ppermute(high, "dp", [(i, i + 2) for i in senders])
        down = lax.ppermute(low, "dp", [(n - 1 - i, n - 3 - i) for i in senders])
        if distance == 2:
            up, down, early = lax.optimization_barrier((up, down, early))
    mine = lax.dynamic_index_in_dim(own, place, 0, keepdims=False).astype(jnp.float32)
    return mine + up.astype(jnp.float32) + down.astype(jnp.float32), early


def dp_total(value):
    n = lax.axis_size("dp")
    shift = 1
    while shift < n:
        value = value + lax.ppermute(value, "dp", swap_pairs(shift, n))
        shift *= 2
    return value


def body(
    images, kernel, layernorm_gain, layernorm_bias, w_expand, w_reduce, layer_scale, cotangent
):
    shape_in = images.shape
    height = shape_in[1]
    breadth = shape_in[2]
    positions = shape_in[0] * height * breadth
    local_chan = shape_in[3]
    image_width = local_chan * lax.axis_size("chan")
    xf = images.astype(jnp.float32)
    conv = depthwise(xf, kernel).reshape(positions, local_chan)
    mean_val = lax.psum(jnp.sum(conv, axis=1), "chan")[:, None] / image_width
    centred_rows = conv - mean_val
    var = lax.psum(jnp.sum(centred_rows * centred_rows, axis=1), "chan")[:, None] / image_width
    inverse_deviation = lax.rsqrt(var + eps)
    standardized_input = centred_rows * inverse_deviation
    normed_output = (standardized_input * layernorm_gain + layernorm_bias).astype(jnp.bfloat16)
    normed_all = chan_gather(normed_output)
    expand_all = lax.all_gather(w_expand, "dp", axis=0, tiled=True)
    pre = jnp.dot(normed_all, expand_all, preferred_element_type=jnp.float32)
    hidden = (pre * normal_cdf(pre)).astype(jnp.bfloat16)
    dyf = cotangent.astype(jnp.float32).reshape(positions, local_chan)
    dbranch = (dyf * layer_scale).astype(jnp.bfloat16)
    dbranch_all = chan_gather(dbranch)
    reduce_part = lax.dot_general(
        dbranch_all, hidden, (((0,), (0,)), ((), ())), preferred_element_type=jnp.float32
    ).astype(jnp.bfloat16)
    reduce_all = lax.all_gather(w_reduce, "dp", axis=1, tiled=True)
    grad_reduce, reduce_all = dp_line_scatter(reduce_part, reduce_all)
    grad_reduce = grad_reduce.T
    dhidden = lax.dot_general(
        dbranch_all, reduce_all, (((1,), (1,)), ((), ())), preferred_element_type=jnp.float32
    )
    slope = normal_cdf(pre) + pre * jnp.exp(-0.5 * pre * pre) / math.sqrt(2.0 * math.pi)
    dpre = (dhidden * slope).astype(jnp.bfloat16)
    expand_part = lax.dot_general(
        normed_all, dpre, (((0,), (0,)), ((), ())), preferred_element_type=jnp.float32
    ).astype(jnp.bfloat16)
    expand_part, dpre, hidden, reduce_all = lax.optimization_barrier(
        (expand_part, dpre, hidden, reduce_all)
    )
    grad_expand = dp_scatter(expand_part).astype(jnp.float32)
    partial_normed = lax.dot_general(
        dpre, expand_all, (((1,), (1,)), ((), ())), preferred_element_type=jnp.float32
    )
    normed_grad = chan_scatter(partial_normed.astype(jnp.bfloat16))
    partial_branch = jnp.dot(hidden, reduce_all, preferred_element_type=jnp.float32)
    branch = chan_scatter(partial_branch.astype(jnp.bfloat16))
    xr = xf.reshape(positions, local_chan)
    output = (xr + layer_scale * branch).astype(jnp.bfloat16).reshape(shape_in)
    scale_part = jnp.sum(dyf * branch, axis=0)
    gain_partial = jnp.sum(normed_grad * standardized_input, axis=0)
    bias_part = jnp.sum(normed_grad, axis=0)
    standardized_grad = normed_grad * layernorm_gain
    first_half, second_half = lax.psum(
        (
            jnp.sum(standardized_grad, axis=1),
            jnp.sum(standardized_grad * standardized_input, axis=1),
        ),
        "chan",
    )
    conv_output_grad = inverse_deviation * (
        standardized_grad
        - first_half[:, None] / image_width
        - standardized_input * (second_half[:, None] / image_width)
    )
    conv_output_grad = conv_output_grad.reshape(shape_in)
    padded = jnp.pad(xf, ((0, 0), (3, 3), (3, 3), (0, 0)))
    dpad = jnp.pad(conv_output_grad, ((0, 0), (3, 3), (3, 3), (0, 0)))
    back = cotangent.astype(jnp.float32)
    kern_rows = []
    for i in range(7):
        tap_row = []
        for j in range(7):
            tap_row.append(
                jnp.sum(
                    padded[:, i : i + height, j : j + breadth, :] * conv_output_grad, axis=(0, 1, 2)
                )
            )
            back = back + dpad[:, 6 - i : 6 - i + height, 6 - j : 6 - j + breadth, :] * kernel[i, j]
        kern_rows.append(jnp.stack(tap_row))
    kernel_part = jnp.stack(kern_rows)
    grad_images = back.astype(jnp.bfloat16)
    small = dp_total(
        jnp.concatenate(
            [
                kernel_part.reshape(-1, local_chan),
                gain_partial[None],
                bias_part[None],
                scale_part[None],
            ]
        )
    )
    taps = kernel_part.shape[0] * kernel_part.shape[1]
    grad_kernel = small[:taps].reshape(kernel_part.shape)
    gain_gradient, grad_bias, grad_scale = small[taps], small[taps + 1], small[taps + 2]
    return (
        output,
        grad_images,
        grad_kernel,
        gain_gradient,
        grad_bias,
        grad_expand,
        grad_reduce,
        grad_scale,
    )


def solution(mesh):
    in_specs = (
        P("dp", None, None, "chan"),
        P(None, None, "chan"),
        P("chan"),
        P("chan"),
        P("dp", "chan"),
        P("chan", "dp"),
        P("chan"),
        P("dp", None, None, "chan"),
    )
    out_specs = (
        P("dp", None, None, "chan"),
        P("dp", None, None, "chan"),
        P(None, None, "chan"),
        P("chan"),
        P("chan"),
        P("dp", "chan"),
        P("chan", "dp"),
        P("chan"),
    )
    return jax.shard_map(body, mesh=mesh, in_specs=in_specs, out_specs=out_specs, check_vma=False)
```
